32 devices in a mesh: ctx: 8 (over z, y), head: 4 (over x, core).
Axes of the slice: x: 2, y: 2, z: 4, core: 2. Of those that a mesh axis runs over, the one named last changes fastest.
Arguments:
- activations: bfloat16 [8192, 2048], P(('ctx', 'head')), may hold values from -6 to 6
- w_query: bfloat16 [2048, 1024], P('ctx', 'head'), may hold values from -0.125 to 0.125
- w_key: bfloat16 [2048, 1024], P('ctx', 'head'), may hold values from -0.125 to 0.125
- w_value: bfloat16 [2048, 2048], P('ctx', 'head'), may hold values from -0.125 to 0.125
- w_zgate: bfloat16 [2048, 2048], P('ctx', 'head'), may hold values from -0.125 to 0.125
- conv_query: bfloat16 [4, 1024], P(None, 'head'), may hold values from -3 to 3
- conv_key: bfloat16 [4, 1024], P(None, 'head'), may hold values from -3 to 3
- conv_value: bfloat16 [4, 2048], P(None, 'head'), may hold values from -3 to 3
- gate_code: int32 [8192, 16], P('ctx', 'head'), may hold values from 0 to 726816
- beta_code: int32 [8192, 16], P('ctx', 'head'), may hold values from 0 to 65536
- norm_gain: float32 [128], replicated, may hold values from 0.1 to 1.9
- w_out: bfloat16 [2048, 2048], P('head', 'ctx'), may hold values from -0.125 to 0.125
Outputs:
- layer_out: bfloat16 [8192, 2048], P(('ctx', 'head'))
The draws below stay inside these ranges and needn't reach their ends.
All inputs are finite; a program needn't handle non-finite values.
Results may differ from the reference program's by a relative error of at most 0.012.
Values may be sent and summed in bfloat16 or wider, within the bound.
A program may use at most 192 MiB of HBM per device.

```python
import jax
import jax.numpy as jnp
from jax import lax

D = 2048
HK = 8
SHARD_OUTPUT_HEAD = 16
DK = 128
DV = 128
KW = 4
SPAN = 64
SEQUENCE_LENGTH = 8192


def head_speeds(key):
    return jax.random.randint(jax.random.fold_in(key, 11), (SHARD_OUTPUT_HEAD,), 0, 2)


def draw_gate_code(key, part):
    speeds = head_speeds(key)
    slow_code = jax.random.randint(jax.random.fold_in(key, 21), (SEQUENCE_LENGTH, SHARD_OUTPUT_HEAD), 0, 1048576 // SEQUENCE_LENGTH + 1)
    fast_code = jax.random.randint(jax.random.fold_in(key, 22), (SEQUENCE_LENGTH, SHARD_OUTPUT_HEAD), 1048576 // 50, 1048576 // 25 + 1)
    picked_group = jax.random.randint(jax.random.fold_in(key, 23), (SEQUENCE_LENGTH, SHARD_OUTPUT_HEAD), 0, SEQUENCE_LENGTH) < 2
    sampled_group_name = jax.random.randint(jax.random.fold_in(key, 24), (SEQUENCE_LENGTH, SHARD_OUTPUT_HEAD), 233017, 726817)
    picked_variant = jnp.where(speeds[None, :] == 1, fast_code, slow_code)
    return jnp.where(picked_group, sampled_group_name, picked_variant).astype(jnp.int32)


def draw_beta_code(key, part):
    speeds = head_speeds(key)
    slow_code = jax.random.randint(jax.random.fold_in(key, 31), (SEQUENCE_LENGTH, SHARD_OUTPUT_HEAD), 0, 65536 * DK // SEQUENCE_LENGTH + 1)
    fast_code = jax.random.randint(jax.random.fold_in(key, 32), (SEQUENCE_LENGTH, SHARD_OUTPUT_HEAD), 16384, 65537)
    return jnp.where(speeds[None, :] == 1, fast_code, slow_code).astype(jnp.int32)


def block_scale(stream_key, shape, pieces, smallest, top_value):
    gain, own = 1.0, jax.random.fold_in(stream_key, 6)
    for dim, blocks in pieces:
        draws = jnp.exp(jax.random.uniform(jax.random.fold_in(own, dim), (blocks,), jnp.float32, smallest / len(pieces), top_value / len(pieces)))
        gain = gain * jnp.repeat(draws, shape[dim] // blocks).reshape([-1 if axis == dim else 1 for axis in range(len(shape))])
    return gain


def bell_draw(rng, dims, scale, reach, split=(), kind=jnp.bfloat16):
    drawn = jax.random.normal(rng, dims, jnp.float32) * scale
    if len(split) > 0:
        drawn = block_scale(rng, dims, split, -0.22, 0.18) * drawn
    return jnp.clip(drawn, min=-reach, max=reach).astype(kind)


def setup_inputs(seed: int = 0) -> dict:
    arg_keys = jax.random.split(jax.random.key(seed), 13)
    return {
        "activations": bell_draw(arg_keys[0], (SEQUENCE_LENGTH, D), 1.0, 6.0, ((0, 32),)),
        "w_query": bell_draw(arg_keys[1], (D, HK * DK), D ** -0.5, 0.125, ((0, 8), (1, 4))),
        "w_key": bell_draw(arg_keys[2], (D, HK * DK), D ** -0.5, 0.125, ((0, 8), (1, 4))),
        "w_value": bell_draw(arg_keys[3], (D, SHARD_OUTPUT_HEAD * DV), D ** -0.5, 0.125, ((0, 8), (1, 4))),
        "w_zgate": bell_draw(arg_keys[4], (D, SHARD_OUTPUT_HEAD * DV), D ** -0.5, 0.125, ((0, 8), (1, 4))),
        "conv_query": bell_draw(arg_keys[5], (KW, HK * DK), KW ** -0.5, 3.0, ((1, 4),)),
        "conv_key": bell_draw(arg_keys[6], (KW, HK * DK), KW ** -0.5, 3.0, ((1, 4),)),
        "conv_value": bell_draw(arg_keys[7], (KW, SHARD_OUTPUT_HEAD * DV), KW ** -0.5, 3.0, ((1, 4),)),
        "gate_code": draw_gate_code(jax.random.fold_in(arg_keys[12], 71), 0),
        "beta_code": draw_beta_code(jax.random.fold_in(arg_keys[12], 71), 0),
        "norm_gain": jnp.clip(1.0 + 0.18 * jax.random.normal(arg_keys[10], (DV,), jnp.float32), 0.1, 1.9),
        "w_out": bell_draw(arg_keys[11], (SHARD_OUTPUT_HEAD * DV, D), (SHARD_OUTPUT_HEAD * DV) ** -0.5, 0.125, ((0, 4), (1, 8))),
    }


def contract(form, left, right):
    return jnp.einsum(form, left, right, precision=lax.Precision.HIGHEST)

def causal_conv(edge_rows, raw_rows, weights):
    tap_count = weights.shape[0]
    joined = jnp.concatenate([edge_rows, raw_rows], 0).astype(jnp.float32)
    length = raw_rows.shape[0]
    summed = jnp.zeros((length, raw_rows.shape[1]), jnp.float32)
    for offset in range(tap_count):
        summed = summed + joined[offset:offset + length] * weights[offset].astype(jnp.float32)
    return jax.nn.silu(summed).astype(jnp.bfloat16)

def span_terms(query_rows, key_rows, value_rows, log_gate, beta_rows):
    cumulated = jnp.cumsum(log_gate, axis=-1)
    length = log_gate.shape[-1]
    key_width = key_rows.shape[-1]
    positions = jnp.arange(length)
    strict_mask = positions[:, None] > positions[None, :]
    incl_mask = positions[:, None] >= positions[None, :]
    differences = cumulated[..., :, None] - cumulated[..., None, :]
    decay_strict = jnp.where(strict_mask, jnp.exp(jnp.where(strict_mask, differences, 0.0)), 0.0)
    decay_incl = jnp.where(incl_mask, jnp.exp(jnp.where(incl_mask, differences, 0.0)), 0.0)
    key_gram = contract('...id,...jd->...ij', key_rows, key_rows)
    mixing = beta_rows[..., :, None] * key_gram * decay_strict
    identity_block = jnp.eye(length, dtype=jnp.float32)
    right_hand = jnp.concatenate([key_rows * (beta_rows * jnp.exp(cumulated))[..., None], value_rows * beta_rows[..., None]], -1)
    solved = jax.scipy.linalg.solve_triangular(identity_block + mixing, right_hand, lower=True, unit_diagonal=True)
    w_block = solved[..., :key_width]
    u_block = solved[..., key_width:]
    tail_decay = jnp.exp(cumulated[..., -1:] - cumulated)
    key_decayed = key_rows * tail_decay[..., None]
    eye_key = jnp.eye(key_width, dtype=jnp.float32)
    transition = jnp.exp(cumulated[..., -1])[..., None, None] * eye_key - contract('...cd,...ce->...de', key_decayed, w_block)
    written = contract('...cd,...ce->...de', key_decayed, u_block)
    scores = contract('...id,...jd->...ij', query_rows, key_rows) * decay_incl
    query_eff = query_rows * jnp.exp(cumulated)[..., None] - contract('...ij,...jd->...id', scores, w_block)
    local_out = contract('...ij,...jd->...id', scores, u_block)
    return (query_eff, local_out, transition, written)

def reference(activations, w_query, w_key, w_value, w_zgate, conv_query, conv_key, conv_value, gate_code, beta_code, norm_gain, w_out):
    query_proj = jnp.dot(activations.astype(jnp.float32), w_query.astype(jnp.float32), preferred_element_type=jnp.float32).astype(jnp.bfloat16)
    key_proj = jnp.dot(activations.astype(jnp.float32), w_key.astype(jnp.float32), preferred_element_type=jnp.float32).astype(jnp.bfloat16)
    value_proj = jnp.dot(activations.astype(jnp.float32), w_value.astype(jnp.float32), preferred_element_type=jnp.float32).astype(jnp.bfloat16)
    zgate_proj = jnp.dot(activations.astype(jnp.float32), w_zgate.astype(jnp.float32), preferred_element_type=jnp.float32).astype(jnp.bfloat16)
    query_conv = causal_conv(jnp.zeros((KW - 1, query_proj.shape[1]), jnp.bfloat16), query_proj, conv_query)
    key_conv = causal_conv(jnp.zeros((KW - 1, key_proj.shape[1]), jnp.bfloat16), key_proj, conv_key)
    convolved_value = causal_conv(jnp.zeros((KW - 1, value_proj.shape[1]), jnp.bfloat16), value_proj, conv_value)
    group_size = SHARD_OUTPUT_HEAD // HK
    blocks = SEQUENCE_LENGTH // SPAN

    def one_head(head_index):
        key_head = (head_index // group_size).astype(jnp.int32)
        query_rows = lax.dynamic_slice_in_dim(query_conv, key_head * DK, DK, 1).astype(jnp.float32)
        key_raw = lax.dynamic_slice_in_dim(key_conv, key_head * DK, DK, 1).astype(jnp.float32)
        key_rows = key_raw / jnp.sqrt(lax.optimization_barrier(jnp.sum(key_raw * key_raw, -1, keepdims=True)) + 1e-06)
        value_rows = lax.dynamic_slice_in_dim(convolved_value, head_index * DV, DV, 1).astype(jnp.float32)
        zgate_rows = lax.dynamic_slice_in_dim(zgate_proj, head_index * DV, DV, 1).astype(jnp.float32)
        log_gate = -lax.dynamic_slice_in_dim(gate_code, head_index, 1, 1)[:, 0].astype(jnp.float32) / 1048576.0
        beta_rows = lax.dynamic_slice_in_dim(beta_code, head_index, 1, 1)[:, 0].astype(jnp.float32) / 65536.0
        query_eff, local_out, transition, written = span_terms(query_rows.reshape(blocks, SPAN, DK), key_rows.reshape(blocks, SPAN, DK), value_rows.reshape(blocks, SPAN, DV), log_gate.reshape(blocks, SPAN), beta_rows.reshape(blocks, SPAN))

        def advance(state_now, step_items):
            query_block, local_block, trans_block, store_segment = step_items
            result = local_block + contract('cd,de->ce', query_block, state_now)
            state_now = contract('de,ef->df', trans_block, state_now) + store_segment
            return (state_now, result)
        start_state = jnp.zeros((DK, DV), jnp.float32)
        unused, core_out = lax.scan(advance, start_state, (query_eff, local_out, transition, written))
        core_out = core_out.reshape(SEQUENCE_LENGTH, DV)
        mean_square = lax.optimization_barrier(jnp.mean(core_out * core_out, -1, keepdims=True))
        normed = core_out * lax.rsqrt(mean_square + 1e-06) * norm_gain * jax.nn.silu(zgate_rows)
        return normed.astype(jnp.bfloat16)
    stacked = lax.map(one_head, jnp.arange(SHARD_OUTPUT_HEAD, dtype=jnp.int32))
    normed_all = jnp.transpose(stacked, (1, 0, 2)).reshape(SEQUENCE_LENGTH, SHARD_OUTPUT_HEAD * DV)
    return jnp.dot(normed_all.astype(jnp.float32), w_out.astype(jnp.float32), preferred_element_type=jnp.float32).astype(jnp.bfloat16)
```

```python
import functools
import jax
import jax.numpy as jnp
from jax import lax
from jax.experimental import pallas as pl
from jax.experimental.pallas import tpu as pltpu
from jax.sharding import PartitionSpec as P

DK = 128
DV = 128
KW = 4
CHUNK = 128
RIM = 16
PAIR = 2
MESH = pl.DeviceIdType.MESH
NN = (((1,), (0,)), ((), ()))
NT = (((1,), (1,)), ((), ()))
BF = jnp.bfloat16
F32 = jnp.float32


def dot(a, b, dims=NN):
    return lax.dot_general(a, b, dims, preferred_element_type=F32)


def silu(x):
    half = 0.5 * x
    return half + half * jnp.tanh(half)


def ring_device(position, n):
    odd = lax.div(position, n // 2)
    return (1 - odd) * (2 * position) + odd * (2 * (n - 1 - position) + 1)


class Stream:
    def __init__(self, n, view, send, recv):
        ctx, head = lax.axis_index("ctx"), lax.axis_index("head")
        odd = lax.rem(ctx, 2)
        position = (1 - odd) * lax.div(ctx, 2) + odd * (n - 1 - lax.div(ctx, 2))
        after = ring_device(lax.rem(position + 1, n), n)
        before = ring_device(lax.rem(position + n - 1, n), n)
        self.reach = n // 2
        self.units = {}
        for s in range(self.reach):
            for way in range(2):
                for half in range(2):
                    if s == self.reach - 1 and half != way:
                        continue
                    owner = ring_device(lax.rem(position + (n - s if way == 0 else s), n), n)
                    index = (s * 2 + way) * 2 + half
                    place = view(owner, half)
                    self.units[s, way, half] = pltpu.make_async_remote_copy(
                        src_ref=place,
                        dst_ref=place,
                        send_sem=send.at[index],
                        recv_sem=recv.at[index],
                        device_id=(after if way == 0 else before, head),
                        device_id_type=MESH,
                    )
        self.owner = lambda s, way: ring_device(lax.rem(position + (n - s if way == 0 else s), n), n)
        self.waited = set()

    def start(self):
        for half in range(2):
            for way in range(2):
                if (0, way, half) in self.units:
                    self.units[0, way, half].start()

    def relay(self, s):
        for half in range(2):
            for way in range(2):
                if (s, way, half) in self.units:
                    self.units[s - 1, way, half].wait_recv()
                    self.waited.add((s - 1, way, half))
                    self.units[s, way, half].start()

    def finish(self):
        for key, unit in self.units.items():
            if key not in self.waited:
                unit.wait_recv()

    def drain(self):
        for unit in self.units.values():
            unit.wait_send()


def unit_inverse(lowers, rows, cols):
    eye = (rows == cols).astype(F32)
    same = (rows >> 3) == (cols >> 3)
    nears = [jnp.where(same, -x, 0.0) for x in lowers]
    firsts = [x.astype(BF) for x in nears]
    powers = [dot(x, x).astype(BF) for x in firsts]
    totals = [eye + x for x in nears]
    totals = [t + dot(t.astype(BF), p) for t, p in zip(totals, powers)]
    powers = [dot(p, p).astype(BF) for p in powers]
    totals = [t + dot(t.astype(BF), p) for t, p in zip(totals, powers)]
    width = 3
    while (1 << width) < CHUNK:
        pair = ((rows >> (width + 1)) == (cols >> (width + 1))) & ((rows >> width) != (cols >> width))
        parts = [t.astype(BF) for t in totals]
        offs = [jnp.where(pair, x, 0.0).astype(BF) for x in lowers]
        mids = [dot(t, o).astype(BF) for t, o in zip(parts, offs)]
        totals = [t - dot(m, p) for t, m, p in zip(totals, mids, parts)]
        width += 1
    return totals


def layer_kernel(
    n, heads, key_heads, group, wide,
    act_ref, wq_ref, wk_ref, wv_ref, wz_ref, wo_ref, cq_ref, ck_ref, cv_ref, gate_ref, beta_ref, gain_ref,
    out_ref,
    act, weight, mix, raw, zed, gates, wu, lhs, rhs, tails, run, core, query, maps, norm, norm_all,
    local_sem, act_send, act_recv, rim_send, rim_recv, ring_send, ring_recv, map_send, map_recv, mix_send, mix_recv, norm_send, norm_recv,
):
    ctx, head = lax.axis_index("ctx"), lax.axis_index("head")
    one = head + 1 - 2 * lax.rem(head, 2)
    two = lax.rem(head + 2, heads)
    three = lax.rem(one + 2, heads)
    rows = act_ref.shape[0]
    length = rows * heads
    depth = wq_ref.shape[0]
    chunks = length // CHUNK
    span = 2 * DK + group * DV

    def weight_view(g):
        def view(owner, half):
            return weight.at[g, pl.ds(pl.multiple_of(owner * depth + half * (depth // 2), depth // 2), depth // 2)]

        return view

    def mix_slot(h, owner, half=None):
        size = mix.shape[2] if wide else wo_ref.shape[0]
        if wide:
            return mix.at[h, owner] if half is None else mix.at[h, owner, pl.ds(half * (size // 2), size // 2)]
        if half is None:
            return mix.at[h, pl.ds(pl.multiple_of(owner * size, size), size)]
        return mix.at[h, pl.ds(pl.multiple_of(owner * size + half * (size // 2), size // 2), size // 2)]

    place = pl.ds(pl.multiple_of(ctx * depth, depth), depth)
    mine = []
    for g in range(key_heads):
        mine.append((wq_ref.at[:, pl.ds(g * DK, DK)], weight.at[g, place, pl.ds(0, DK)]))
        mine.append((wk_ref.at[:, pl.ds(g * DK, DK)], weight.at[g, place, pl.ds(DK, DK)]))
        mine.append((wv_ref.at[:, pl.ds(g * group * DV, group * DV)], weight.at[g, place, pl.ds(2 * DK, group * DV)]))
    mine.append((wz_ref, weight.at[key_heads, place]))
    mine.append((wo_ref, mix_slot(head, ctx)))
    block = lambda h, sub: act.at[pl.ds(pl.multiple_of(RIM + h * rows + sub * (rows // PAIR), 16), rows // PAIR)]
    piece = lambda sub: act_ref.at[pl.ds(sub * (rows // PAIR), rows // PAIR)]
    for sub in range(PAIR):
        mine.append((piece(sub), block(head, sub)))
    mine = [pltpu.make_async_copy(a, b, local_sem.at[i]) for i, (a, b) in enumerate(mine)]
    for copy in mine:
        copy.start()

    barrier = pltpu.get_barrier_semaphore()
    odd = lax.rem(ctx, 2)
    position = (1 - odd) * lax.div(ctx, 2) + odd * (n - 1 - lax.div(ctx, 2))
    for step in (1, n - 1):
        other = ring_device(lax.rem(position + step, n), n)
        pl.semaphore_signal(barrier, inc=1, device_id=(other, head), device_id_type=MESH)
    for peer in (one, two, three):
        pl.semaphore_signal(barrier, inc=1, device_id=(ctx, peer), device_id_type=MESH)
    gives_rim = (head == heads - 1) & (ctx < n - 1)

    @pl.when(ctx > 0)
    def _():
        pl.semaphore_signal(barrier, inc=1, device_id=(ctx - 1, heads - 1), device_id_type=MESH)

    pl.semaphore_wait(barrier, 5 + heads * gives_rim.astype(jnp.int32))

    def to_peer(src, dst, index, peer):
        return pltpu.make_async_remote_copy(
            src_ref=src, dst_ref=dst, send_sem=act_send.at[index], recv_sem=act_recv.at[index], device_id=(ctx, peer), device_id_type=MESH
        )

    across = [to_peer(piece(s), block(head, s), s, two) for s in range(PAIR)]
    beside = [to_peer(piece(s), block(head, s), PAIR + s, one) for s in range(PAIR)]
    onward = [to_peer(block(two, s), block(two, s), 2 * PAIR + s, one) for s in range(PAIR)]
    rims = [
        pltpu.make_async_remote_copy(
            src_ref=act_ref.at[pl.ds(rows - RIM, RIM)],
            dst_ref=act.at[pl.ds(0, RIM)],
            send_sem=rim_send.at[h],
            recv_sem=rim_recv,
            device_id=(lax.rem(ctx + 1, n), h),
            device_id_type=MESH,
        )
        for h in range(heads)
    ]
    streams = [Stream(n, weight_view(g), ring_send.at[g], ring_recv.at[g]) for g in range(key_heads + 1)]
    mixes = Stream(n, lambda owner, half: mix_slot(head, owner, half), ring_send.at[key_heads + 1], ring_recv.at[key_heads + 1])
    map_streams = [
        Stream(n, lambda owner, half, g=g: maps.at[g, owner, pl.ds(half * group * DK // 2, group * DK // 2)], map_send.at[g], map_recv.at[g])
        for g in range(key_heads)
    ]

    @pl.when(gives_rim)
    def _():
        for copy in rims:
            copy.start()

    for copy in across:
        copy.start()
    for copy in beside:
        copy.start()
    for copy in mine:
        copy.wait()

    @pl.when(ctx == 0)
    def _():
        act[0:RIM, :] = jnp.zeros((RIM, act.shape[1]), BF)

    streams[0].start()

    iota = lambda dim: lax.broadcasted_iota(jnp.int32, (CHUNK, CHUNK), dim)
    tri = (iota(0) <= iota(1)).astype(BF)
    decays = gate_ref[...].astype(F32) * (-1.0 / 1048576.0)
    betas = beta_ref[...].astype(F32) * (1.0 / 65536.0)
    values = key_heads * group
    stacked = jnp.concatenate([decays[:, c * CHUNK : (c + 1) * CHUNK] for c in range(chunks)], 0)
    g1 = stacked.astype(BF)
    rest = stacked - g1.astype(F32)
    g2 = rest.astype(BF)
    g3 = (rest - g2.astype(F32)).astype(BF)
    sums = dot(g1, tri) + (dot(g2, tri) + dot(g3, tri))
    for g in range(key_heads):
        for c in range(chunks):
            for r in range(group):
                h = g * group + r
                gates[g, c, r : r + 1, :] = sums[c * values + h : c * values + h + 1, :]
                gates[g, c, group + r : group + r + 1, :] = betas[h : h + 1, c * CHUNK : (c + 1) * CHUNK]
            gates[g, c, 2 * group :, :] = jnp.zeros((8 - 2 * group, CHUNK), F32)

    def relay_all(stream):
        for s in range(1, stream.reach):
            stream.relay(s)

    for s in range(1, streams[0].reach):
        streams[0].relay(s)
    for stream in streams[1:]:
        stream.start()
        relay_all(stream)
    mixes.start()
    relay_all(mixes)
    for a, b in zip(across, onward):
        a.wait_recv()
        b.start()

    @pl.when(ctx > 0)
    def _():
        rims[0].wait_recv()

    for copy in beside + onward:
        copy.wait_recv()
    for stream in streams + [mixes]:
        stream.finish()

    def mix_copy(src, index, peer):
        return pltpu.make_async_remote_copy(
            src_ref=src, dst_ref=src, send_sem=mix_send.at[index], recv_sem=mix_recv.at[index], device_id=(ctx, peer), device_id_type=MESH
        )

    mix_across = mix_copy(mix.at[head], 0, two)
    mix_beside = mix_copy(mix.at[head], 1, one)
    mix_onward = mix_copy(mix.at[two], 2, one)
    mix_across.start()
    mix_beside.start()

    def project(g, store):
        tile = (length + RIM) // 5

        def body(m, carry):
            start = pl.multiple_of(m * tile, 16)
            store(start, tile, dot(act[pl.ds(start, tile), :], weight[g]))
            return carry

        lax.fori_loop(0, 5, body, 0)

    def store_raw(start, tile, value):
        raw[pl.ds(start, tile), :] = value

    def store_zed(start, tile, value):
        zed[pl.ds(start, tile), :] = silu(value)

    def within(g, chunk_list):
        row_id, col_id = iota(0), iota(1)
        strict, incl = row_id > col_id, row_id >= col_id
        taps = [
            jnp.concatenate(
                [
                    cq_ref[j : j + 1, g * DK : (g + 1) * DK],
                    ck_ref[j : j + 1, g * DK : (g + 1) * DK],
                    cv_ref[j : j + 1, g * group * DV : (g + 1) * group * DV],
                ],
                1,
            ).astype(F32)
            for j in range(KW)
        ]
        items, lowers = [], []
        for c in chunk_list:
            x = raw[pl.ds(pl.multiple_of(c * CHUNK, CHUNK), CHUNK + RIM), :]
            acc = x[RIM - KW + 1 : RIM - KW + 1 + CHUNK] * taps[0]
            for j in range(1, KW):
                acc = acc + x[RIM - KW + 1 + j : RIM - KW + 1 + j + CHUNK] * taps[j]
            conv = silu(acc)
            q, k = conv[:, :DK], conv[:, DK : 2 * DK]
            khat = k * lax.rsqrt(jnp.sum(k * k, -1, keepdims=True) + 1e-06)
            turned = jnp.transpose(khat)
            both = jnp.concatenate([q.astype(BF), khat.astype(BF)], 0)
            pairs = dot(both, turned.astype(BF))
            qk, gram = pairs[:CHUNK], pairs[CHUNK:]
            info = gates[g, c]
            info_t = jnp.transpose(info)
            for r in range(group):
                row, col = info[r : r + 1, :], info_t[:, r : r + 1]
                beta = info_t[:, group + r : group + r + 1]
                decay = jnp.exp(jnp.minimum(col - row, 0.0))
                lowers.append(jnp.where(strict, beta * gram * decay, 0.0))
                grown = jnp.exp(col)
                v = conv[:, 2 * DK + r * DV : 2 * DK + (r + 1) * DV]
                right = jnp.concatenate([khat * (beta * grown), v * beta], 1).astype(BF)
                lhs[c, r, :, :DK] = (q * grown).astype(BF)
                lhs[c, r, :, DK:] = jnp.where(incl, qk * decay, 0.0).astype(BF)
                tails[c, r] = (turned * jnp.exp(row[:, CHUNK - 1 :] - row)).astype(BF)
                items.append((c, r, right))
        for (c, r, right), inverse in zip(items, unit_inverse(lowers, row_id, col_id)):
            wu[c, r] = dot(inverse.astype(BF), right).astype(BF)

    def advance(g):
        eye = (iota(0) == iota(1)).astype(F32)
        for r in range(group):
            run[r, :, :DK] = eye
            run[r, :, DK:] = jnp.zeros((DK, DV), F32)

        def body(c, carry):
            states = [run[r] for r in range(group)]
            parts = [s.astype(BF) for s in states]
            news = []
            for r in range(group):
                rhs[c, r, :DK, :] = parts[r]
                got = wu[c, r]
                taken = dot(got[:, :DK], parts[r])
                y = jnp.concatenate([-taken[:, :DK], got[:, DK:].astype(F32) - taken[:, DK:]], 1)
                news.append(y.astype(BF))
            for r in range(group):
                rhs[c, r, DK:, :] = news[r]
                last = jnp.exp(gates[g, c, r : r + 1, CHUNK - 1 :])
                run[r] = last * states[r] + dot(tails[c, r], news[r])
            return carry

        lax.fori_loop(0, chunks, body, 0)
        for r in range(group):
            maps[g, ctx, r * DK : (r + 1) * DK, :] = run[r].astype(BF)

    def outputs(g):
        def body(c, carry):
            place = pl.ds(pl.multiple_of(c * CHUNK, CHUNK), CHUNK)
            for r in range(group):
                got = dot(lhs[c, r], rhs[c, r])
                query[g, place, r * DK : (r + 1) * DK] = got[:, :DK].astype(BF)
                core[g, place, r * DV : (r + 1) * DV] = got[:, DK:]
            return carry

        lax.fori_loop(0, chunks, body, 0)

    def close(g):
        def hop(p, states):
            news = []
            for r in range(group):
                high = states[r].astype(BF)
                low = (states[r] - high.astype(F32)).astype(BF)
                both = maps[g, p, r * DK : (r + 1) * DK, :]
                trans = both[:, :DK]
                news.append(dot(trans, high) + dot(trans, low) + both[:, DK:].astype(F32))
            return tuple(news)

        states = lax.fori_loop(0, ctx, hop, tuple(jnp.zeros((DK, DV), F32) for _ in range(group)))
        states = [s.astype(BF) for s in states]
        gain = gain_ref[...]

        def body(d, carry):
            place = pl.ds(pl.multiple_of(d * rows, rows), rows)
            gate_rows = pl.ds(pl.multiple_of(RIM + d * rows, 16), rows)
            for r in range(group):
                h = g * group + r
                full = core[g, place, r * DV : (r + 1) * DV] + dot(query[g, place, r * DK : (r + 1) * DK], states[r])
                mean = jnp.mean(full * full, -1, keepdims=True)
                value = full * lax.rsqrt(mean + 1e-06) * gain * zed[gate_rows, h * DV : (h + 1) * DV]
                norm[g, d, :, r * DV : (r + 1) * DV] = value.astype(BF)
            return carry

        lax.fori_loop(0, heads, body, 0)

    def share(g):
        copies = [
            pltpu.make_async_remote_copy(
                src_ref=norm.at[g, peer],
                dst_ref=norm_all.at[g, head],
                send_sem=norm_send.at[g, i],
                recv_sem=norm_recv.at[g, i],
                device_id=(ctx, peer),
                device_id_type=MESH,
            )
            for i, peer in enumerate((two, three, one))
        ]
        for copy in copies:
            copy.start()
        keep = pltpu.make_async_copy(norm.at[g, head], norm_all.at[g, head], local_sem.at[g])
        keep.start()
        return copies, keep

    shared = []
    for g in range(key_heads):
        project(g, store_raw)

        def body(i, carry):
            within(g, [2 * i, 2 * i + 1])
            return carry

        lax.fori_loop(0, chunks // 2, body, 0)
        advance(g)
        map_streams[g].start()
        outputs(g)
        relay_all(map_streams[g])
    project(key_heads, store_zed)
    mix_across.wait_recv()
    mix_onward.start()
    for g in range(key_heads):
        map_streams[g].finish()
        close(g)
        shared.append(share(g))
    mix_beside.wait_recv()
    mix_onward.wait_recv()
    for copies, keep in shared:
        for copy in copies:
            copy.wait_recv()
        keep.wait()

    width = group * DV
    out_tile = mix.shape[3] if wide else 256

    def last(p, carry):
        total = jnp.zeros((rows, out_tile), F32)
        for h in range(heads):
            for g in range(key_heads):
                left = norm_all[g, h]
                if wide:
                    total = total + dot(left, mix[h, p, g * width : (g + 1) * width, :])
                else:
                    right = mix[h, pl.ds(pl.multiple_of(p * out_tile, out_tile), out_tile), g * width : (g + 1) * width]
                    total = total + dot(left, right, NT)
        out_ref[:, pl.ds(pl.multiple_of(p * out_tile, out_tile), out_tile)] = total.astype(BF)
        return carry

    lax.fori_loop(0, out_ref.shape[1] // out_tile, last, 0)

    for copy in across + beside + onward + [mix_across, mix_beside, mix_onward]:
        copy.wait_send()

    @pl.when(gives_rim)
    def _():
        for copy in rims:
            copy.wait_send()

    for stream in streams + [mixes] + map_streams:
        stream.drain()
    for copies, keep in shared:
        for copy in copies:
            copy.wait_send()


def shards(activations, w_query, w_key, w_value, w_zgate, conv_query, conv_key, conv_value, gate_code, beta_code, norm_gain, w_out):
    n, heads = lax.axis_size("ctx"), lax.axis_size("head")
    rows, width = activations.shape
    length = rows * heads
    values = gate_code.shape[1]
    key_heads = w_query.shape[1] // DK
    group = values // key_heads
    span = 2 * DK + group * DV
    depth = w_query.shape[0]
    wide = w_out.shape[1] % 256 == 0
    wo = w_out if wide else w_out.T
    mix_shape = (heads, n) + w_out.shape if wide else (heads, n * w_out.shape[1], w_out.shape[0])
    chunks = length // CHUNK
    any_ref = pl.BlockSpec(memory_space=pl.ANY)
    vmem = pl.BlockSpec(memory_space=pltpu.VMEM)
    units = 4 * (n // 2)
    dma = pltpu.SemaphoreType.DMA
    return pl.pallas_call(
        functools.partial(layer_kernel, n, heads, key_heads, group, wide),
        in_specs=[any_ref] * 6 + [vmem] * 6,
        out_specs=vmem,
        out_shape=jax.ShapeDtypeStruct((rows, n * w_out.shape[1]), BF),
        scratch_shapes=[
            pltpu.VMEM((RIM + length, width), BF),
            pltpu.VMEM((key_heads + 1, n * depth, span), BF),
            pltpu.VMEM(mix_shape, BF),
            pltpu.VMEM((RIM + length, span), F32),
            pltpu.VMEM((RIM + length, values * DV), F32),
            pltpu.VMEM((key_heads, chunks, 8, CHUNK), F32),
            pltpu.VMEM((chunks, group, CHUNK, DK + DV), BF),
            pltpu.VMEM((chunks, group, CHUNK, DK + CHUNK), BF),
            pltpu.VMEM((chunks, group, DK + CHUNK, DK + DV), BF),
            pltpu.VMEM((chunks, group, DK, CHUNK), BF),
            pltpu.VMEM((group, DK, DK + DV), F32),
            pltpu.VMEM((key_heads, length, group * DV), F32),
            pltpu.VMEM((key_heads, length, group * DK), BF),
            pltpu.VMEM((key_heads, n, group * DK, DK + DV), BF),
            pltpu.VMEM((key_heads, heads, rows, group * DV), BF),
            pltpu.VMEM((key_heads, heads, rows, group * DV), BF),
            dma((3 * key_heads + 2 + PAIR,)),
            dma((3 * PAIR,)),
            dma((3 * PAIR,)),
            dma((heads,)),
            dma,
            dma((key_heads + 2, units)),
            dma((key_heads + 2, units)),
            dma((key_heads, units)),
            dma((key_heads, units)),
            dma((3,)),
            dma((3,)),
            dma((key_heads, heads - 1)),
            dma((key_heads, heads - 1)),
        ],
        compiler_params=pltpu.CompilerParams(collective_id=0, has_side_effects=True, vmem_limit_bytes=63 * 1024 * 1024),
        name="layer",
    )(
        activations, w_query, w_key, w_value, w_zgate, wo, conv_query, conv_key, conv_value,
        gate_code.T, beta_code.T, norm_gain.reshape(1, DV),
    )


def solution(mesh):
    return jax.shard_map(
        shards,
        mesh=mesh,
        in_specs=(
            P(("ctx", "head"), None),
            P("ctx", "head"),
            P("ctx", "head"),
            P("ctx", "head"),
            P("ctx", "head"),
            P(None, "head"),
            P(None, "head"),
            P(None, "head"),
            P("ctx", "head"),
            P("ctx", "head"),
            P(),
            P("head", "ctx"),
        ),
        out_specs=P(("ctx", "head"), None),
        check_vma=False,
    )
```

```python
import functools
import jax
import jax.numpy as jnp
from jax import lax
from jax.experimental import pallas as pl
from jax.experimental.pallas import tpu as pltpu
from jax.sharding import PartitionSpec as P

DK = 128
DV = 128
KW = 4
CHUNK = 128
RIM = 16
PAIR = 2
MESH = pl.DeviceIdType.MESH
NN = (((1,), (0,)), ((), ()))
NT = (((1,), (1,)), ((), ()))
BF = jnp.bfloat16
F32 = jnp.float32


def dot(a, b, dims=NN):
    return lax.dot_general(a, b, dims, preferred_element_type=F32)


def silu(x):
    half = 0.5 * x
    return half + half * jnp.tanh(half)


def ring_device(position, n):
    odd = lax.div(position, n // 2)
    return (1 - odd) * (2 * position) + odd * (2 * (n - 1 - position) + 1)


class Stream:
    def __init__(self, n, view, send, recv):
        ctx, head = lax.axis_index("ctx"), lax.axis_index("head")
        odd = lax.rem(ctx, 2)
        position = (1 - odd) * lax.div(ctx, 2) + odd * (n - 1 - lax.div(ctx, 2))
        after = ring_device(lax.rem(position + 1, n), n)
        before = ring_device(lax.rem(position + n - 1, n), n)
        self.reach = n // 2
        self.units = {}
        for s in range(self.reach):
            for way in range(2):
                for half in range(2):
                    if s == self.reach - 1 and half != way:
                        continue
                    owner = ring_device(lax.rem(position + (n - s if way == 0 else s), n), n)
                    index = (s * 2 + way) * 2 + half
                    place = view(owner, half)
                    self.units[s, way, half] = pltpu.make_async_remote_copy(
                        src_ref=place,
                        dst_ref=place,
                        send_sem=send.at[index],
                        recv_sem=recv.at[index],
                        device_id=(after if way == 0 else before, head),
                        device_id_type=MESH,
                    )
        self.arrived = lambda s, way: ring_device(lax.rem(position + (n - s - 1 if way == 0 else s + 1), n), n)
        self.waited = set()

    def start(self):
        for half in range(2):
            for way in range(2):
                if (0, way, half) in self.units:
                    self.units[0, way, half].start()

    def relay(self, s):
        for half in range(2):
            for way in range(2):
                if (s, way, half) in self.units:
                    self.units[s - 1, way, half].wait_recv()
                    self.waited.add((s - 1, way, half))
                    self.units[s, way, half].start()

    def bundle(self, k, parts=3, then=lambda s: None):
        for s in range(1, self.reach):
            if (s - 1) * parts // max(self.reach - 1, 1) == k:
                self.relay(s)
                then(s - 1)

    def settle(self, s):
        for key, unit in self.units.items():
            if key[0] == s and key not in self.waited:
                unit.wait_recv()
                self.waited.add(key)

    def finish(self):
        for s in range(self.reach):
            self.settle(s)

    def drain(self):
        for unit in self.units.values():
            unit.wait_send()


def unit_inverse(lowers, rows, cols):
    eye = (rows == cols).astype(F32)
    same = (rows >> 3) == (cols >> 3)
    nears = [jnp.where(same, -x, 0.0) for x in lowers]
    firsts = [x.astype(BF) for x in nears]
    powers = [dot(x, x).astype(BF) for x in firsts]
    totals = [eye + x for x in nears]
    totals = [t + dot(t.astype(BF), p) for t, p in zip(totals, powers)]
    powers = [dot(p, p).astype(BF) for p in powers]
    totals = [t + dot(t.astype(BF), p) for t, p in zip(totals, powers)]
    width = 3
    while (1 << width) < CHUNK:
        pair = ((rows >> (width + 1)) == (cols >> (width + 1))) & ((rows >> width) != (cols >> width))
        parts = [t.astype(BF) for t in totals]
        offs = [jnp.where(pair, x, 0.0).astype(BF) for x in lowers]
        mids = [dot(t, o).astype(BF) for t, o in zip(parts, offs)]
        totals = [t - dot(m, p) for t, m, p in zip(totals, mids, parts)]
        width += 1
    return totals


def layer_kernel(
    n, heads, key_heads, group, wide,
    act_ref, wq_ref, wk_ref, wv_ref, wz_ref, wo_ref, cq_ref, ck_ref, cv_ref, gate_ref, beta_ref, gain_ref,
    out_ref,
    act, weight, zweight, mix, raw, zed, gates, wu, lhs, rhs, tails, run, core, query, enter, leave, norm, norm_all,
    local_sem, act_send, act_recv, rim_send, rim_recv, ring_send, ring_recv, pass_send, pass_recv, mix_send, mix_recv, norm_send, norm_recv,
):
    ctx, head = lax.axis_index("ctx"), lax.axis_index("head")
    one = head + 1 - 2 * lax.rem(head, 2)
    two = lax.rem(head + 2, heads)
    three = lax.rem(one + 2, heads)
    rows = act_ref.shape[0]
    length = rows * heads
    depth = wq_ref.shape[0]
    chunks = length // CHUNK
    span = 2 * DK + group * DV

    def weight_view(buffer, g):
        def view(owner, half):
            return buffer.at[g, pl.ds(pl.multiple_of(owner * depth + half * (depth // 2), depth // 2), depth // 2)]

        return view

    def mix_slot(h, owner, half=None):
        size = mix.shape[2] if wide else wo_ref.shape[0]
        if wide:
            return mix.at[h, owner] if half is None else mix.at[h, owner, pl.ds(half * (size // 2), size // 2)]
        if half is None:
            return mix.at[h, pl.ds(pl.multiple_of(owner * size, size), size)]
        return mix.at[h, pl.ds(pl.multiple_of(owner * size + half * (size // 2), size // 2), size // 2)]

    place = pl.ds(pl.multiple_of(ctx * depth, depth), depth)
    mine = []
    for g in range(key_heads):
        mine.append((wq_ref.at[:, pl.ds(g * DK, DK)], weight.at[g, place, pl.ds(0, DK)]))
        mine.append((wk_ref.at[:, pl.ds(g * DK, DK)], weight.at[g, place, pl.ds(DK, DK)]))
        mine.append((wv_ref.at[:, pl.ds(g * group * DV, group * DV)], weight.at[g, place, pl.ds(2 * DK, group * DV)]))
    for g in range(key_heads):
        mine.append((wz_ref.at[:, pl.ds(g * group * DV, group * DV)], zweight.at[g, place]))
    mine.append((wo_ref, mix_slot(head, ctx)))
    block = lambda h, sub: act.at[pl.ds(pl.multiple_of(RIM + h * rows + sub * (rows // PAIR), 16), rows // PAIR)]
    piece = lambda sub: act_ref.at[pl.ds(sub * (rows // PAIR), rows // PAIR)]
    for sub in range(PAIR):
        mine.append((piece(sub), block(head, sub)))
    mine = [pltpu.make_async_copy(a, b, local_sem.at[i]) for i, (a, b) in enumerate(mine)]
    for copy in mine:
        copy.start()

    barrier = pltpu.get_barrier_semaphore()
    odd = lax.rem(ctx, 2)
    position = (1 - odd) * lax.div(ctx, 2) + odd * (n - 1 - lax.div(ctx, 2))
    for step in (1, n - 1):
        other = ring_device(lax.rem(position + step, n), n)
        pl.semaphore_signal(barrier, inc=1, device_id=(other, head), device_id_type=MESH)
    for peer in (one, two, three):
        pl.semaphore_signal(barrier, inc=1, device_id=(ctx, peer), device_id_type=MESH)
    gives_rim = (head == heads - 1) & (ctx < n - 1)

    @pl.when(ctx > 0)
    def _():
        pl.semaphore_signal(barrier, inc=1, device_id=(ctx - 1, heads - 1), device_id_type=MESH)

    @pl.when(ctx > 0)
    def _():
        pl.semaphore_signal(barrier, inc=1, device_id=(ctx - 1, head), device_id_type=MESH)

    @pl.when(ctx < n - 1)
    def _():
        pl.semaphore_signal(barrier, inc=1, device_id=(ctx + 1, head), device_id_type=MESH)

    inner = (ctx > 0).astype(jnp.int32) + (ctx < n - 1).astype(jnp.int32)
    pl.semaphore_wait(barrier, 5 + inner + heads * gives_rim.astype(jnp.int32))

    def to_peer(src, dst, index, peer):
        return pltpu.make_async_remote_copy(
            src_ref=src, dst_ref=dst, send_sem=act_send.at[index], recv_sem=act_recv.at[index], device_id=(ctx, peer), device_id_type=MESH
        )

    across = [to_peer(piece(s), block(head, s), s, two) for s in range(PAIR)]
    beside = [to_peer(piece(s), block(head, s), PAIR + s, one) for s in range(PAIR)]
    onward = [to_peer(block(two, s), block(two, s), 2 * PAIR + s, one) for s in range(PAIR)]
    rims = [
        pltpu.make_async_remote_copy(
            src_ref=act_ref.at[pl.ds(rows - RIM, RIM)],
            dst_ref=act.at[pl.ds(0, RIM)],
            send_sem=rim_send.at[h],
            recv_sem=rim_recv,
            device_id=(lax.rem(ctx + 1, n), h),
            device_id_type=MESH,
        )
        for h in range(heads)
    ]
    stream = lambda view, i: Stream(n, view, ring_send.at[i], ring_recv.at[i])
    streams = [stream(weight_view(weight, g), g) for g in range(key_heads)]
    zeds = [stream(weight_view(zweight, g), key_heads + g) for g in range(key_heads)]
    mixes = stream(lambda owner, half: mix_slot(head, owner, half), 2 * key_heads)

    @pl.when(gives_rim)
    def _():
        for copy in rims:
            copy.start()

    for copy in across:
        copy.start()
    for copy in beside:
        copy.start()
    for copy in mine:
        copy.wait()

    @pl.when(ctx == 0)
    def _():
        act[0:RIM, :] = jnp.zeros((RIM, act.shape[1]), BF)

    streams[0].start()

    iota = lambda dim: lax.broadcasted_iota(jnp.int32, (CHUNK, CHUNK), dim)
    tri = (iota(0) <= iota(1)).astype(BF)
    decays = gate_ref[...].astype(F32) * (-1.0 / 1048576.0)
    betas = beta_ref[...].astype(F32) * (1.0 / 65536.0)
    values = key_heads * group
    stacked = jnp.concatenate([decays[:, c * CHUNK : (c + 1) * CHUNK] for c in range(chunks)], 0)
    g1 = stacked.astype(BF)
    rest = stacked - g1.astype(F32)
    g2 = rest.astype(BF)
    g3 = (rest - g2.astype(F32)).astype(BF)
    sums = dot(g1, tri) + (dot(g2, tri) + dot(g3, tri))
    for g in range(key_heads):
        for c in range(chunks):
            for r in range(group):
                h = g * group + r
                gates[g, c, r : r + 1, :] = sums[c * values + h : c * values + h + 1, :]
                gates[g, c, group + r : group + r + 1, :] = betas[h : h + 1, c * CHUNK : (c + 1) * CHUNK]
            gates[g, c, 2 * group :, :] = jnp.zeros((8 - 2 * group, CHUNK), F32)

    def mix_copy(h, owner, half, kind, index, peer):
        place = mix_slot(h, owner, half)
        return pltpu.make_async_remote_copy(
            src_ref=place, dst_ref=place, send_sem=mix_send.at[kind, index], recv_sem=mix_recv.at[kind, index], device_id=(ctx, peer), device_id_type=MESH
        )

    def mix_group(keys):
        found = []
        for owner, half, index in keys:
            found.append(
                (
                    mix_copy(head, owner, half, 0, index, two),
                    mix_copy(head, owner, half, 1, index, one),
                    mix_copy(two, owner, half, 2, index, one),
                )
            )
        return found

    mix_sets = [mix_group([(ctx, half, half) for half in range(2)])]
    for s in range(mixes.reach):
        keys = [(mixes.arrived(s, way), half, 2 + (s * 2 + way) * 2 + half) for half in range(2) for way in range(2) if (s, way, half) in mixes.units]
        mix_sets.append(mix_group(keys))

    def mix_forward(s):
        for across_copy, beside_copy, _ in mix_sets[s]:
            across_copy.start()
            beside_copy.start()

    def mix_onward(s):
        for across_copy, _, onward_copy in mix_sets[s]:
            across_copy.wait_recv()
            onward_copy.start()

    onward_done = [0]

    def mix_catch_up(share, shares):
        stop = (mixes.reach + 1) * share // shares
        while onward_done[0] < stop:
            mix_onward(onward_done[0])
            onward_done[0] += 1

    def hooked(count, body, hooks):
        def step(i, carry):
            for j, hook in hooks.items():
                pl.when(i == j)(hook)
            body(i)
            return carry

        lax.fori_loop(0, count, step, 0)

    def project(matrix, store):
        tile = (length + RIM) // 5

        def body(m, carry):
            start = pl.multiple_of(m * tile, 16)
            store(start, tile, dot(act[pl.ds(start, tile), :], matrix[...]))
            return carry

        lax.fori_loop(0, 5, body, 0)

    def store_raw(start, tile, value):
        raw[pl.ds(start, tile), :] = value

    def store_zed(g):
        def store(start, tile, value):
            zed[g, pl.ds(start, tile), :] = silu(value)

        return store

    def within(g, chunk_list):
        row_id, col_id = iota(0), iota(1)
        strict, incl = row_id > col_id, row_id >= col_id
        taps = [
            jnp.concatenate(
                [
                    cq_ref[j : j + 1, g * DK : (g + 1) * DK],
                    ck_ref[j : j + 1, g * DK : (g + 1) * DK],
                    cv_ref[j : j + 1, g * group * DV : (g + 1) * group * DV],
                ],
                1,
            ).astype(F32)
            for j in range(KW)
        ]
        items, lowers = [], []
        for c in chunk_list:
            x = raw[pl.ds(pl.multiple_of(c * CHUNK, CHUNK), CHUNK + RIM), :]
            acc = x[RIM - KW + 1 : RIM - KW + 1 + CHUNK] * taps[0]
            for j in range(1, KW):
                acc = acc + x[RIM - KW + 1 + j : RIM - KW + 1 + j + CHUNK] * taps[j]
            conv = silu(acc)
            q, k = conv[:, :DK], conv[:, DK : 2 * DK]
            khat = k * lax.rsqrt(jnp.sum(k * k, -1, keepdims=True) + 1e-06)
            turned = jnp.transpose(khat)
            both = jnp.concatenate([q.astype(BF), khat.astype(BF)], 0)
            pairs = dot(both, turned.astype(BF))
            qk, gram = pairs[:CHUNK], pairs[CHUNK:]
            info = gates[g, c]
            info_t = jnp.transpose(info)
            for r in range(group):
                row, col = info[r : r + 1, :], info_t[:, r : r + 1]
                beta = info_t[:, group + r : group + r + 1]
                decay = jnp.exp(jnp.minimum(col - row, 0.0))
                lowers.append(jnp.where(strict, beta * gram * decay, 0.0))
                grown = jnp.exp(col)
                v = conv[:, 2 * DK + r * DV : 2 * DK + (r + 1) * DV]
                right = jnp.concatenate([khat * (beta * grown), v * beta], 1).astype(BF)
                lhs[c, r, :, :DK] = (q * grown).astype(BF)
                lhs[c, r, :, DK:] = jnp.where(incl, qk * decay, 0.0).astype(BF)
                tails[c, r] = (turned * jnp.exp(row[:, CHUNK - 1 :] - row)).astype(BF)
                items.append((c, r, right))
        for (c, r, right), inverse in zip(items, unit_inverse(lowers, row_id, col_id)):
            wu[c, r] = dot(inverse.astype(BF), right).astype(BF)

    def advance(g):
        eye = (iota(0) == iota(1)).astype(F32)
        for r in range(group):
            run[g, r, :, :DK] = eye
            run[g, r, :, DK:] = jnp.zeros((DK, DV), F32)

        def body(c, carry):
            states = [run[g, r] for r in range(group)]
            parts = [s.astype(BF) for s in states]
            news = []
            for r in range(group):
                rhs[c, r, :DK, :] = parts[r]
                got = wu[c, r]
                taken = dot(got[:, :DK], parts[r])
                y = jnp.concatenate([-taken[:, :DK], got[:, DK:].astype(F32) - taken[:, DK:]], 1)
                news.append(y.astype(BF))
            for r in range(group):
                rhs[c, r, DK:, :] = news[r]
                last = jnp.exp(gates[g, c, r : r + 1, CHUNK - 1 :])
                run[g, r] = last * states[r] + dot(tails[c, r], news[r])
            return carry

        lax.fori_loop(0, chunks, body, 0)

    passes = [
        pltpu.make_async_remote_copy(
            src_ref=leave.at[g],
            dst_ref=enter.at[g],
            send_sem=pass_send.at[g],
            recv_sem=pass_recv.at[g],
            device_id=(lax.rem(ctx + 1, n), head),
            device_id_type=MESH,
        )
        for g in range(key_heads)
    ]

    def chain(g, point, points=8):
        @pl.when(lax.div(ctx * points, n) == point)
        def _():
            @pl.when(ctx == 0)
            def _():
                enter[g] = jnp.zeros(enter.shape[1:], BF)

            @pl.when(ctx > 0)
            def _():
                passes[g].wait_recv()

            @pl.when(ctx < n - 1)
            def _():
                for r in range(group):
                    both = run[g, r]
                    leave[g, r] = (dot(both[:, :DK].astype(BF), enter[g, r]) + both[:, DK:]).astype(BF)
                passes[g].start()

    def outputs(g):
        def body(c, carry):
            place = pl.ds(pl.multiple_of(c * CHUNK, CHUNK), CHUNK)
            for r in range(group):
                got = dot(lhs[c, r], rhs[c, r])
                query[g, place, r * DK : (r + 1) * DK] = got[:, :DK].astype(BF)
                core[g, place, r * DV : (r + 1) * DV] = got[:, DK:]
            return carry

        lax.fori_loop(0, chunks, body, 0)

    def close(g):
        states = [enter[g, r] for r in range(group)]
        gain = gain_ref[...]

        def body(d, carry):
            place = pl.ds(pl.multiple_of(d * rows, rows), rows)
            gate_rows = pl.ds(pl.multiple_of(RIM + d * rows, 16), rows)
            for r in range(group):
                full = core[g, place, r * DV : (r + 1) * DV] + dot(query[g, place, r * DK : (r + 1) * DK], states[r])
                mean = jnp.mean(full * full, -1, keepdims=True)
                value = full * lax.rsqrt(mean + 1e-06) * gain * zed[g, gate_rows, r * DV : (r + 1) * DV]
                norm[g, d, :, r * DV : (r + 1) * DV] = value.astype(BF)
            return carry

        lax.fori_loop(0, heads, body, 0)

    def share(g):
        copies = [
            pltpu.make_async_remote_copy(
                src_ref=norm.at[g, peer],
                dst_ref=norm_all.at[g, head],
                send_sem=norm_send.at[g, i],
                recv_sem=norm_recv.at[g, i],
                device_id=(ctx, peer),
                device_id_type=MESH,
            )
            for i, peer in enumerate((two, three, one))
        ]
        for copy in copies:
            copy.start()
        keep = pltpu.make_async_copy(norm.at[g, head], norm_all.at[g, head], local_sem.at[g])
        keep.start()
        return copies, keep

    first, later = streams[0], streams[1:]
    queue = later + [mixes] + zeds
    def pass_mix(s):
        mixes.settle(s)
        mix_forward(s + 1)

    notes = {id(mixes): pass_mix}
    steps = []
    for i, one_stream in enumerate([first] + queue):
        for k in range(3):
            steps.append((one_stream, k, queue[i] if k == 2 and i < len(queue) else None))
    steps.reverse()

    def step():
        if steps:
            one_stream, k, following = steps.pop()
            one_stream.bundle(k, 3, notes.get(id(one_stream), lambda s: None))
            if following is not None:
                following.start()

    step()
    step()
    across[0].wait_recv()
    onward[0].start()
    step()
    across[1].wait_recv()
    onward[1].start()
    mix_forward(0)

    @pl.when(ctx > 0)
    def _():
        rims[0].wait_recv()

    for copy in beside + onward:
        copy.wait_recv()
    first.finish()

    shared = []
    for g in range(key_heads):
        if g > 0:
            streams[g].finish()
        project(weight.at[g], store_raw)
        step()
        if g > 0:
            chain(g - 1, 1)

        def body(i):
            within(g, [2 * i, 2 * i + 1])

        def hook(k):
            def run_hook():
                if g > 0:
                    chain(g - 1, 2 + k)
                if k % 2 == 1:
                    step()

            return run_hook

        hooked(chunks // 2, body, {k: hook(k) for k in range(4)})
        advance(g)
        if g > 0:
            chain(g - 1, 6)
        chain(g, 0)
        outputs(g)
        if g > 0:
            chain(g - 1, 7)
    last_group = key_heads - 1
    mixes.finish()
    mix_forward(mixes.reach)
    mix_catch_up(1, 4)
    step()
    chain(last_group, 1)
    step()
    chain(last_group, 2)
    step()
    mix_catch_up(2, 4)
    chain(last_group, 3)
    for g in range(key_heads):
        zeds[g].finish()
        project(zweight.at[g], store_zed(g))
        if g < last_group:
            step()
            chain(last_group, 4)
            close(g)
            shared.append(share(g))
            step()
            chain(last_group, 5)
            mix_catch_up(3, 4)
            step()
            chain(last_group, 6)
    chain(last_group, 7)
    close(last_group)
    shared.append(share(last_group))
    while steps:
        step()
    mix_catch_up(4, 4)
    for group_copies in mix_sets:
        for _, beside_copy, onward_copy in group_copies:
            beside_copy.wait_recv()
            onward_copy.wait_recv()
    for copies, keep in shared:
        for copy in copies:
            copy.wait_recv()
        keep.wait()

    width = group * DV
    out_tile = mix.shape[3] if wide else 256

    def last(p, carry):
        total = jnp.zeros((rows, out_tile), F32)
        for h in range(heads):
            for g in range(key_heads):
                left = norm_all[g, h]
                if wide:
                    total = total + dot(left, mix[h, p, g * width : (g + 1) * width, :])
                else:
                    right = mix[h, pl.ds(pl.multiple_of(p * out_tile, out_tile), out_tile), g * width : (g + 1) * width]
                    total = total + dot(left, right, NT)
        out_ref[:, pl.ds(pl.multiple_of(p * out_tile, out_tile), out_tile)] = total.astype(BF)
        return carry

    lax.fori_loop(0, out_ref.shape[1] // out_tile, last, 0)

    for copy in across + beside + onward:
        copy.wait_send()
    for group_copies in mix_sets:
        for copies in group_copies:
            for copy in copies:
                copy.wait_send()

    @pl.when(ctx < n - 1)
    def _():
        for copy in passes:
            copy.wait_send()

    @pl.when(gives_rim)
    def _():
        for copy in rims:
            copy.wait_send()

    for one_stream in [first] + queue:
        one_stream.drain()
    for copies, keep in shared:
        for copy in copies:
            copy.wait_send()


def shards(activations, w_query, w_key, w_value, w_zgate, conv_query, conv_key, conv_value, gate_code, beta_code, norm_gain, w_out):
    n, heads = lax.axis_size("ctx"), lax.axis_size("head")
    rows, width = activations.shape
    length = rows * heads
    values = gate_code.shape[1]
    key_heads = w_query.shape[1] // DK
    group = values // key_heads
    span = 2 * DK + group * DV
    depth = w_query.shape[0]
    wide = w_out.shape[1] % 256 == 0
    wo = w_out if wide else w_out.T
    mix_shape = (heads, n) + w_out.shape if wide else (heads, n * w_out.shape[1], w_out.shape[0])
    chunks = length // CHUNK
    any_ref = pl.BlockSpec(memory_space=pl.ANY)
    vmem = pl.BlockSpec(memory_space=pltpu.VMEM)
    units = 4 * (n // 2)
    dma = pltpu.SemaphoreType.DMA
    return pl.pallas_call(
        functools.partial(layer_kernel, n, heads, key_heads, group, wide),
        in_specs=[any_ref] * 6 + [vmem] * 6,
        out_specs=vmem,
        out_shape=jax.ShapeDtypeStruct((rows, n * w_out.shape[1]), BF),
        scratch_shapes=[
            pltpu.VMEM((RIM + length, width), BF),
            pltpu.VMEM((key_heads, n * depth, span), BF),
            pltpu.VMEM((key_heads, n * depth, group * DV), BF),
            pltpu.VMEM(mix_shape, BF),
            pltpu.VMEM((RIM + length, span), F32),
            pltpu.VMEM((key_heads, RIM + length, group * DV), F32),
            pltpu.VMEM((key_heads, chunks, 8, CHUNK), F32),
            pltpu.VMEM((chunks, group, CHUNK, DK + DV), BF),
            pltpu.VMEM((chunks, group, CHUNK, DK + CHUNK), BF),
            pltpu.VMEM((chunks, group, DK + CHUNK, DK + DV), BF),
            pltpu.VMEM((chunks, group, DK, CHUNK), BF),
            pltpu.VMEM((key_heads, group, DK, DK + DV), F32),
            pltpu.VMEM((key_heads, length, group * DV), F32),
            pltpu.VMEM((key_heads, length, group * DK), BF),
            pltpu.VMEM((key_heads, group, DK, DV), BF),
            pltpu.VMEM((key_heads, group, DK, DV), BF),
            pltpu.VMEM((key_heads, heads, rows, group * DV), BF),
            pltpu.VMEM((key_heads, heads, rows, group * DV), BF),
            dma((4 * key_heads + 1 + PAIR,)),
            dma((3 * PAIR,)),
            dma((3 * PAIR,)),
            dma((heads,)),
            dma,
            dma((2 * key_heads + 1, units)),
            dma((2 * key_heads + 1, units)),
            dma((key_heads,)),
            dma((key_heads,)),
            dma((3, units + 2)),
            dma((3, units + 2)),
            dma((key_heads, heads - 1)),
            dma((key_heads, heads - 1)),
        ],
        compiler_params=pltpu.CompilerParams(collective_id=0, has_side_effects=True, vmem_limit_bytes=63 * 1024 * 1024),
        name="layer",
    )(
        activations, w_query, w_key, w_value, w_zgate, wo, conv_query, conv_key, conv_value,
        gate_code.T, beta_code.T, norm_gain.reshape(1, DV),
    )


def solution(mesh):
    return jax.shard_map(
        shards,
        mesh=mesh,
        in_specs=(
            P(("ctx", "head"), None),
            P("ctx", "head"),
            P("ctx", "head"),
            P("ctx", "head"),
            P("ctx", "head"),
            P(None, "head"),
            P(None, "head"),
            P(None, "head"),
            P("ctx", "head"),
            P("ctx", "head"),
            P(),
            P("head", "ctx"),
        ),
        out_specs=P(("ctx", "head"), None),
        check_vma=False,
    )
```
